256 devices in a mesh: blk: 128 (over z, y, x_hi, core), rep: 2 (over x_lo).
Axes of the slice: x: 4 (x_hi: 2, x_lo: 2; x = x_hi * 2 + x_lo), y: 4, z: 8, core: 2. Of those that a mesh axis runs over, the one named last changes fastest.
Arguments:
- inputs: bfloat16 [32768, 5120], P(('blk', 'rep')), may hold values from -6 to 6
- upstream: bfloat16 [32768, 5120], P(('blk', 'rep')), may hold values from -6 to 6
- w_gate_t: bfloat16 [27648, 5120], P('blk', 'rep'), may hold values from -0.078125 to 0.078125
- w_up_t: bfloat16 [27648, 5120], P('blk', 'rep'), may hold values from -0.078125 to 0.078125
- w_down: bfloat16 [27648, 5120], P('blk', 'rep'), may hold values from -0.3125 to 0.3125
Outputs:
- grad_inputs: bfloat16 [32768, 5120], P(('blk', 'rep'))
- grad_gate_t: bfloat16 [27648, 5120], P('blk', 'rep')
- grad_up_t: bfloat16 [27648, 5120], P('blk', 'rep')
- grad_down: bfloat16 [27648, 5120], P('blk', 'rep')
The draws below stay inside these ranges and needn't reach their ends.
All inputs are finite; a program needn't handle non-finite values.
Results may differ from the reference program's by a relative error of at most 0.0049.
Values may be sent and summed in bfloat16 or wider, within the bound.
No kernel may reach another device: no remote copies, remote signals or barrier semaphores. Data moves between devices by JAX's collectives and lax.ppermute only.
A program may use at most 128 MiB of HBM per device.

```python
import jax
import jax.numpy as jnp
from jax import lax

D = 5120
HID_DEV = 216
VISITS = 2
TOK_DEV = 128
FF = 27648
TOKENS = 32768
N_BLK = 128
N_REP = 2


def block_scale(key, extent, shards, smallest, largest):
    loudness = 1.0
    for dim, shards_of in shards:
        draws = jax.random.uniform(jax.random.fold_in(jax.random.fold_in(key, 6), dim), (shards_of,), jnp.float32, smallest / len(shards), largest / len(shards))
        loudness = loudness * jnp.repeat(jnp.exp(draws), extent[dim] // shards_of).reshape((-1,) + (1,) * (len(extent) - 1 - dim))
    return loudness


def scatter_about(key, dims, spread, bound, shards=(), kind=jnp.bfloat16):
    result = spread * jax.random.normal(key, dims, jnp.float32)
    if shards:
        result = result * block_scale(key, dims, shards, -0.22, 0.18)
    return jnp.clip(result, -bound, bound).astype(kind)


def setup_inputs(seed: int = 0) -> dict:
    seeds = jax.random.split(jax.random.key(seed), 6)
    inputs = scatter_about(seeds[0], (TOKENS, D), 1.0, 6.0, ((0, 256),))
    upstream = scatter_about(seeds[1], (TOKENS, D), 1.0, 6.0, ((0, 256),))
    w_gate_t = scatter_about(seeds[2], (FF, D), D ** -0.5, 0.078125, ((0, 128), (1, 2)))
    w_up_t = scatter_about(seeds[3], (FF, D), D ** -0.5, 0.078125, ((0, 128), (1, 2)))
    w_down = scatter_about(seeds[4], (FF, D), (VISITS * HID_DEV) ** -0.5, 0.3125, ((0, 128), (1, 2)))
    return dict(inputs=inputs, upstream=upstream, w_gate_t=w_gate_t, w_up_t=w_up_t, w_down=w_down)


def visit_block(group_in, group_up, gate_rows, up_rows, down_rows):
    last = (((1,), (1,)), ((), ()))
    pre_gate = lax.dot_general(group_in, gate_rows, last, preferred_element_type=jnp.float32)
    pre_up = lax.dot_general(group_in, up_rows, last, preferred_element_type=jnp.float32)
    grad_act = lax.dot_general(group_up, down_rows, last, preferred_element_type=jnp.float32)
    sigmoid_h = jax.nn.sigmoid(pre_gate)
    silu_h = pre_gate * sigmoid_h
    activated = (silu_h * pre_up).astype(jnp.bfloat16)
    grad_pre_gate = (grad_act * pre_up * sigmoid_h * (1.0 + pre_gate * (1.0 - sigmoid_h))).astype(jnp.bfloat16)
    grad_pre_up = (grad_act * silu_h).astype(jnp.bfloat16)
    partial_in = jnp.dot(grad_pre_gate, gate_rows, preferred_element_type=jnp.float32)
    partial_in = partial_in + jnp.dot(grad_pre_up, up_rows, preferred_element_type=jnp.float32)
    contract = (((0,), (0,)), ((), ()))
    block_gate = lax.dot_general(grad_pre_gate, group_in, contract, preferred_element_type=jnp.float32)
    block_up = lax.dot_general(grad_pre_up, group_in, contract, preferred_element_type=jnp.float32)
    block_down = lax.dot_general(activated, group_up, contract, preferred_element_type=jnp.float32)
    return partial_in, (block_gate, block_up, block_down)


def reference(inputs, upstream, w_gate_t, w_up_t, w_down):
    rows_group = TOK_DEV * N_REP

    def one_block(input_grads, block_num):
        row_first = (block_num * HID_DEV).astype(jnp.int32)
        gate_rows = lax.dynamic_slice_in_dim(w_gate_t, row_first, HID_DEV, 0)
        up_rows = lax.dynamic_slice_in_dim(w_up_t, row_first, HID_DEV, 0)
        down_rows = lax.dynamic_slice_in_dim(w_down, row_first, HID_DEV, 0)
        sums = None
        for offset in range(VISITS):
            row_group = ((block_num + offset) % N_BLK).astype(jnp.int32)
            row_start = (row_group * rows_group).astype(jnp.int32)
            group_in = lax.dynamic_slice_in_dim(inputs, row_start, rows_group, 0)
            group_up = lax.dynamic_slice_in_dim(upstream, row_start, rows_group, 0)
            partial_in, block_grads = visit_block(group_in, group_up, gate_rows, up_rows, down_rows)
            current = lax.dynamic_slice_in_dim(input_grads, row_start, rows_group, 0)
            input_grads = lax.dynamic_update_slice_in_dim(input_grads, current + partial_in, row_start, 0)
            sums = block_grads if sums is None else jax.tree.map(jnp.add, sums, block_grads)
        return input_grads, sums

    start_grads = jnp.zeros((TOKENS, D), jnp.float32)
    input_grads, stacked = lax.scan(one_block, start_grads, jnp.arange(N_BLK, dtype=jnp.int32))

    def unstack(blocks):
        return blocks.reshape(FF, D).astype(jnp.bfloat16)

    return (input_grads.astype(jnp.bfloat16), unstack(stacked[0]), unstack(stacked[1]), unstack(stacked[2]))
```

```python
import jax
import jax.numpy as jnp
from jax import lax
from jax.sharding import PartitionSpec as P

BF = jnp.bfloat16
F32 = jnp.float32
AXES = ("blk", "rep")


def routes(n_blk):
    def at(b, r):
        return (b % n_blk) * 2 + r

    every = [(b, r) for b in range(n_blk) for r in (0, 1)]
    return {
        "swap": [(at(b, r), at(b, 1 - r)) for b, r in every],
        "back": [(at(b, r), at(b - 1, r)) for b, r in every],
        "back_flip_even": [(at(b, r), at(b - 1, 1 - r)) for b, r in every if b % 2 == 0],
        "back_odd": [(at(b, r), at(b - 1, r)) for b, r in every if b % 2 == 1],
        "fwd": [(at(b, r), at(b + 1, r)) for b, r in every],
        "fwd_flip": [(at(b, r), at(b + 1, 1 - r)) for b, r in every],
    }


def dot_last(a, b):
    return lax.dot_general(a, b, (((1,), (1,)), ((), ())), preferred_element_type=F32)


def dot_first(a, b):
    return lax.dot_general(a, b, (((0,), (0,)), ((), ())), preferred_element_type=F32)


def pre(x_own, x_oth, g_own, g_oth, gate_up, down):
    x = jnp.concatenate([x_own, x_oth], 0)
    g = jnp.concatenate([g_own, g_oth], 0)
    return x, g, jnp.concatenate([dot_last(x, gate_up), dot_last(g, down)], 1)


def swapped_halves(p):
    n = p.shape[0] // 2
    return jnp.concatenate([p[n:], p[:n]], 0)


def activate(s, hid):
    pre_gate, pre_up, grad_act = s[:, :hid], s[:, hid : 2 * hid], s[:, 2 * hid :]
    sig = jax.nn.sigmoid(pre_gate)
    silu = pre_gate * sig
    act = (silu * pre_up).astype(BF)
    dgate = (grad_act * pre_up * sig * (1.0 + pre_gate * (1.0 - sig))).astype(BF)
    dup = (grad_act * silu).astype(BF)
    return act, dgate, dup


def solution(mesh):
    n_blk = mesh.shape["blk"]
    route = routes(n_blk)

    def go(value, name):
        return lax.ppermute(value, AXES, route[name])

    def per_device(inputs, upstream, w_gate_t, w_up_t, w_down):
        rows, width = inputs.shape
        half = width // 2
        hid = w_down.shape[0]
        rep = lax.axis_index("rep")
        own, oth = rep * half, (1 - rep) * half
        cut = lambda a, at: lax.dynamic_slice(a, (0, at), (rows, half))
        x_own, x_snd = cut(inputs, own), cut(inputs, oth)
        g_own, g_snd = cut(upstream, own), cut(upstream, oth)
        x_oth, g_oth = go(x_snd, "swap"), go(g_snd, "swap")
        x2_oth_e, g2_oth_e = go(x_snd, "back_flip_even"), go(g_snd, "back_flip_even")
        x2_own, g2_own = go(x_own, "back"), go(g_own, "back")
        x2_oth = x2_oth_e + go(x_oth, "back_odd")
        g2_oth = g2_oth_e + go(g_oth, "back_odd")
        gate_up = jnp.concatenate([w_gate_t, w_up_t], 0)

        def visit(xo, xx, go_, gx):
            x, g, p = pre(xo, xx, go_, gx, gate_up, w_down)
            s = p + go(swapped_halves(p).astype(BF), "swap").astype(F32)
            act, dgate, dup = activate(s, hid)
            d = jnp.concatenate([dgate, dup], 1)
            partial = jnp.dot(d, gate_up, preferred_element_type=F32)
            return partial, (dot_first(d, x), dot_first(act, g))

        part1, grads1 = visit(x_own, x_oth, g_own, g_oth)
        other1 = go(part1[rows:].astype(BF), "swap")
        part2, grads2 = visit(x2_own, x2_oth, g2_own, g2_oth)
        part2 = part2.astype(BF)
        own2 = go(part2[:rows], "fwd")
        other2 = go(part2[rows:], "fwd_flip")
        d_own = (part1[:rows] + own2.astype(F32)).astype(BF)
        d_oth = (other1.astype(F32) + other2.astype(F32)).astype(BF)
        d_in = jnp.where(
            rep == 0,
            jnp.concatenate([d_own, d_oth], 1),
            jnp.concatenate([d_oth, d_own], 1),
        )
        gu = (grads1[0] + grads2[0]).astype(BF)
        dn = (grads1[1] + grads2[1]).astype(BF)
        return d_in, gu[:hid], gu[hid:], dn

    tokens, weights = P(AXES, None), P("blk", "rep")
    return jax.shard_map(
        per_device,
        mesh=mesh,
        in_specs=(tokens, tokens, weights, weights, weights),
        out_specs=(tokens, weights, weights, weights),
        check_vma=False,
    )
```

```python
import functools

import jax
import jax.numpy as jnp
from jax import lax
from jax.experimental import pallas as pl
from jax.experimental.pallas import tpu as pltpu
from jax.sharding import PartitionSpec as P

BF = jnp.bfloat16
F32 = jnp.float32
AXES = ("blk", "rep")
LAST = (((1,), (1,)), ((), ()))
IN_VMEM = pl.BlockSpec(memory_space=pltpu.VMEM)
IN_SMEM = pl.BlockSpec(memory_space=pltpu.SMEM)


def routes(n_blk):
    def at(b, r):
        return (b % n_blk) * 2 + r

    every = [(b, r) for b in range(n_blk) for r in (0, 1)]
    return {
        "swap": [(at(b, r), at(b, 1 - r)) for b, r in every],
        "back": [(at(b, r), at(b - 1, r)) for b, r in every],
        "back_flip": [(at(b, r), at(b - 1, r if b % 2 else 1 - r)) for b, r in every],
        "same_chip": [(at(b, r), at(b ^ 1, r)) for b, r in every],
        "fwd": [(at(b, r), at(b + 1, r)) for b, r in every],
        "fwd_flip": [(at(b, r), at(b + 1, 1 - r if b % 2 else r)) for b, r in every],
        "swap_even": [(at(b, r), at(b, 1 - r)) for b, r in every if b % 2 == 0],
        "swap_odd": [(at(b, r), at(b, 1 - r)) for b, r in every if b % 2 == 1],
    }


def call(body, args, outs, flops, scratch=(), scalars=0):
    shapes = [jax.ShapeDtypeStruct(s, t) for s, t in outs]
    nbytes = sum(a.size * a.dtype.itemsize for a in (*args, *shapes))
    return pl.pallas_call(
        body,
        in_specs=[IN_SMEM] * scalars + [IN_VMEM] * (len(args) - scalars),
        out_specs=[IN_VMEM] * len(shapes),
        out_shape=shapes,
        scratch_shapes=list(scratch),
        compiler_params=pltpu.CompilerParams(vmem_limit_bytes=nbytes + (4 << 20)),
        cost_estimate=pl.CostEstimate(flops=flops, bytes_accessed=nbytes, transcendentals=0),
    )(*args)


def pre1_body(t, wg, wu, wd, out, out16):
    rows = t.shape[0] // 2
    x, g = t[:rows], t[rows:]
    for i, (w, v) in enumerate(((wg, x), (wu, x), (wd, g))):
        s = lax.dot_general(w[...], v, LAST, preferred_element_type=F32)
        out[i] = s
        out16[i] = s.astype(BF)


def pre1(tokens, weights):
    rows, width = tokens.shape
    hid = weights[0].shape[0]
    shape = (3, hid, rows // 2)
    return call(
        pre1_body, (tokens, *weights), [(shape, F32), (shape, BF)], 3 * rows * width * hid
    )


def pre2_body(odd, own, by_link, by_chip, wg, wu, wd, out, out16, oth):
    rows = own.shape[0] // 2

    @pl.when(odd[0] == 1)
    def _():
        oth[...] = by_link[...]

    @pl.when(odd[0] == 0)
    def _():
        oth[...] = by_chip[...]

    x = jnp.concatenate([own[:rows], oth[:rows]], 0)
    g = jnp.concatenate([own[rows:], oth[rows:]], 0)
    for i, (w, t) in enumerate(((wg, x), (wu, x), (wd, g))):
        s = lax.dot_general(w[...], t, LAST, preferred_element_type=F32)
        out[i] = s
        out16[i, :, :rows] = s[:, rows:].astype(BF)
        out16[i, :, rows:] = s[:, :rows].astype(BF)


def pre2(odd, own, by_link, by_chip, weights):
    rows, width = own.shape
    hid = weights[0].shape[0]
    shape = (3, hid, rows)
    return call(
        pre2_body,
        (odd, own, by_link, by_chip, *weights),
        [(shape, F32), (shape, BF), ((rows, width), BF)],
        6 * rows * width * hid,
        scalars=1,
    )


def act_body(pieces, chunks, *refs):
    ps, rs = refs[:pieces], refs[pieces : 2 * pieces]
    wg, wu, d = refs[2 * pieces : 2 * pieces + 3]
    own, oth, *more = refs[2 * pieces + 3 : -1]
    turned = refs[-1]
    at = 0
    for p, r in zip(ps, rs):
        gate = p[0] + r[0].astype(F32)
        up = p[1] + r[1].astype(F32)
        ga = p[2] + r[2].astype(F32)
        sig = 1.0 / (1.0 + jnp.exp(-gate))
        silu = gate * sig
        dgate = ga * up * sig * (1.0 + gate * (1.0 - sig))
        dup = ga * silu
        part = pl.ds(at, p.shape[2])
        d[0, :, part] = (silu * up).astype(BF)
        d[1, :, part] = dgate.astype(BF)
        d[2, :, part] = dup.astype(BF)
        turned[0, part, :] = dgate.T.astype(BF)
        turned[1, part, :] = dup.T.astype(BF)
        at += p.shape[2]
    rows, width = own.shape
    n = width // chunks

    @pl.loop(0, chunks)
    def _(c):
        cols = pl.ds(pl.multiple_of(c * n, n), n)
        s = jnp.dot(turned[0], wg[:, cols], preferred_element_type=F32)
        s += jnp.dot(turned[1], wu[:, cols], preferred_element_type=F32)
        own[:, cols] = s[:rows].astype(own.dtype)
        oth[:, cols] = s[rows:].astype(oth.dtype)
        for m in more:
            m[:, cols] = s[rows:].astype(m.dtype)


def act(ps, rs, wg, wu, kinds):
    hid, width = wg.shape
    total = sum(p.shape[2] for p in ps)
    rows = total // 2
    return call(
        functools.partial(act_body, len(ps), 5),
        (*ps, *rs, wg, wu),
        [((3, hid, total), BF)] + [((rows, width), t) for t in kinds],
        8 * rows * hid * width,
        scratch=[pltpu.VMEM((2, total, hid), BF)],
    )


def dw_body(chunks, d1, d2, *refs):
    tokens, outs = refs[:4], refs[4:]
    n = outs[0].shape[1] // chunks
    rows = tokens[0].shape[0] // 2

    @pl.loop(0, chunks)
    def _(c):
        cols = pl.ds(pl.multiple_of(c * n, n), n)
        x = jnp.concatenate([r[:rows, cols] for r in tokens], 0)
        g = jnp.concatenate([r[rows:, cols] for r in tokens], 0)
        for i, out, t in ((1, outs[0], x), (2, outs[1], x), (0, outs[2], g)):
            d = jnp.concatenate([d1[i], d2[i]], 1)
            out[:, cols] = jnp.dot(d, t, preferred_element_type=F32).astype(BF)


def dw(d1, d2, tokens):
    hid = d1.shape[1]
    rows, width = tokens[0].shape
    return call(
        functools.partial(dw_body, 5),
        (d1, d2, *tokens),
        [((hid, width), BF)] * 3,
        12 * rows * hid * width,
    )


def add_body(a, b, out):
    out[...] = (a[...] + b[...].astype(F32)).astype(BF)


def last_body(where, own1, own2, left, flip, s, out):
    half = own1.shape[1]
    own = pl.ds(pl.multiple_of(where[1] * half, 128), half)
    oth = pl.ds(pl.multiple_of((1 - where[1]) * half, 128), half)
    out[:, own] = (own1[...] + own2[...].astype(F32)).astype(BF)

    @pl.when(where[0] == 1)
    def _():
        out[:, oth] = s[...]

    @pl.when(where[0] == 0)
    def _():
        out[:, oth] = (left[...].astype(F32) + flip[...].astype(F32)).astype(BF)


def solution(mesh):
    route = routes(mesh.shape["blk"])

    def go(value, name):
        return lax.ppermute(value, AXES, route[name])

    def steps(inputs, upstream, w_gate_t, w_up_t, w_down):
        rows, width = inputs.shape
        half = width // 2
        weights = (w_gate_t, w_up_t, w_down)
        rep = lax.axis_index("rep").astype(jnp.int32)
        odd = (lax.axis_index("blk") % 2).astype(jnp.int32)

        def cut(a, b, at):
            return jnp.concatenate([lax.dynamic_slice(v, (0, at), (rows, half)) for v in (a, b)], 0)

        mine = cut(*lax.optimization_barrier((inputs, upstream)), rep * half)
        send = cut(inputs, upstream, (1 - rep) * half)
        theirs = go(send, "swap")
        by_link = go(send, "back_flip")
        p1_own, p1_own16 = pre1(mine, weights)
        r1_oth = go(p1_own16, "swap")
        mine2 = go(mine, "back")
        p1_oth, p1_oth16 = pre1(theirs, weights)
        r1_own = go(p1_oth16, "swap")
        by_chip = go(theirs, "same_chip")
        d1, own1, oth1_16, oth1 = act(
            (p1_own, p1_oth), (r1_own, r1_oth), w_gate_t, w_up_t, (F32, BF, F32)
        )
        left = go(oth1_16, "swap_even")
        p2, p2_16, theirs2 = pre2(odd.reshape(1), mine2, by_link, by_chip, weights)
        r2 = go(p2_16, "swap")
        d2, own2, oth2 = act((p2,), (r2,), w_gate_t, w_up_t, (BF, BF))
        oth2_chip = go(oth2, "same_chip")
        own2_home = go(own2, "fwd")
        flip = go(oth2, "fwd_flip")
        (s,) = call(add_body, (oth1, oth2_chip), [((rows, half), BF)], rows * half)
        s_odd = go(s, "swap_odd")
        gg, gu, gd = dw(d1, d2, (mine, theirs, mine2, theirs2))
        (d_in,) = call(
            last_body,
            (jnp.stack([odd, rep]), own1, own2_home, left, flip, s_odd),
            [((rows, width), BF)],
            2 * rows * width,
            scalars=1,
        )
        return d_in, gg, gu, gd

    tokens, weights = P(AXES, None), P("blk", "rep")
    return jax.shard_map(
        steps,
        mesh=mesh,
        in_specs=(tokens, tokens, weights, weights, weights),
        out_specs=(tokens, weights, weights, weights),
        check_vma=False,
    )
```

```python
import functools

import jax
import jax.numpy as jnp
from jax import lax
from jax.experimental import pallas as pl
from jax.experimental.pallas import tpu as pltpu
from jax.sharding import PartitionSpec as P

BF = jnp.bfloat16
F32 = jnp.float32
AXES = ("blk", "rep")
LAST = (((1,), (1,)), ((), ()))
IN_VMEM = pl.BlockSpec(memory_space=pltpu.VMEM)
IN_SMEM = pl.BlockSpec(memory_space=pltpu.SMEM)
IN_PLACE = pl.BlockSpec(memory_space=pltpu.HBM)


def routes(n_blk):
    def at(b, r):
        return (b % n_blk) * 2 + r

    every = [(b, r) for b in range(n_blk) for r in (0, 1)]
    return {
        "swap": [(at(b, r), at(b, 1 - r)) for b, r in every],
        "back": [(at(b, r), at(b - 1, r)) for b, r in every],
        "back_flip": [(at(b, r), at(b - 1, r if b % 2 else 1 - r)) for b, r in every],
        "same_chip": [(at(b, r), at(b ^ 1, r)) for b, r in every],
        "fwd": [(at(b, r), at(b + 1, r)) for b, r in every],
        "fwd_flip": [(at(b, r), at(b + 1, 1 - r)) for b, r in every],
        "swap_even": [(at(b, r), at(b, 1 - r)) for b, r in every if b % 2 == 0],
    }


def call(body, args, outs, flops, scratch=(), scalars=0, raw=0):
    shapes = [jax.ShapeDtypeStruct(s, k) for s, k in outs]
    nbytes = sum(a.size * a.dtype.itemsize for a in (*args, *shapes))
    specs = [IN_SMEM] * scalars + [IN_PLACE] * raw + [IN_VMEM] * (len(args) - scalars - raw)
    return pl.pallas_call(
        body,
        in_specs=specs,
        out_specs=[IN_VMEM] * len(shapes),
        out_shape=shapes,
        scratch_shapes=list(scratch),
        compiler_params=pltpu.CompilerParams(vmem_limit_bytes=nbytes + (4 << 20)),
        cost_estimate=pl.CostEstimate(flops=flops, bytes_accessed=nbytes, transcendentals=0),
    )(*args)


def pre_body(picks, *refs):
    n = max(picks) + 1
    tokens, ws, (out, out16) = refs[:n], refs[n:-2], refs[-2:]
    for i, (w, k) in enumerate(zip(ws, picks)):
        s = lax.dot_general(w[...], tokens[k][...], LAST, preferred_element_type=F32)
        out[i] = s
        out16[i] = s.astype(BF)


def pre(tokens, picks, weights):
    hid, width = weights[0].shape
    rows = tokens[0].shape[0]
    shape = (len(weights), hid, rows)
    return call(
        functools.partial(pre_body, picks),
        (*tokens, *weights),
        [(shape, F32), (shape, BF)],
        2 * len(weights) * rows * width * hid,
    )


def pick_copies(odd, sources, buf, sems):
    rows = sources[0].shape[0]
    for i in range(2):
        dst = buf.at[pl.ds(i * rows, rows)]

        @pl.when(odd[0] == 1)
        def _():
            pltpu.make_async_copy(sources[i], dst, sems.at[i]).start()

        @pl.when(odd[0] == 0)
        def _():
            pltpu.make_async_copy(sources[2 + i], dst, sems.at[i]).start()


def pick_wait(sources, buf, sems, i):
    rows = sources[0].shape[0]
    pltpu.make_async_copy(sources[i], buf.at[pl.ds(i * rows, rows)], sems.at[i]).wait()


def pre2oth_body(odd, *refs):
    sources, (wg, wu, wd, out, out16, buf, sems) = refs[:4], refs[4:]
    rows = sources[0].shape[0]
    pick_copies(odd, sources, buf, sems)
    for i, (w, p) in enumerate(((wg, 0), (wu, 0), (wd, 1))):
        if i != 1:
            pick_wait(sources, buf, sems, p)
        t = buf[p * rows : (p + 1) * rows]
        s = lax.dot_general(w[...], t, LAST, preferred_element_type=F32)
        out[i] = s
        out16[i] = s.astype(BF)


def pre2oth(odd, sources, weights):
    rows, width = sources[0].shape
    hid = weights[0].shape[0]
    shape = (3, hid, rows)
    return call(
        pre2oth_body,
        (odd, *sources, *weights),
        [(shape, F32), (shape, BF)],
        6 * rows * width * hid,
        scratch=[pltpu.VMEM((2 * rows, width), BF), pltpu.SemaphoreType.DMA((2,))],
        scalars=1,
        raw=4,
    )


def act_body(pieces, chunks, joined, *refs):
    if joined:
        keep, extra, *refs = refs
    wg, wu, d, own, oth, turned = refs[-6:]
    at = 0
    for ps, rs in pieces:
        gate, up, ga = (refs[i][j] + refs[k][m].astype(F32) for (i, j), (k, m) in zip(ps, rs))
        sig = 1.0 / (1.0 + jnp.exp(-gate))
        silu = gate * sig
        dgate = ga * up * sig * (1.0 + gate * (1.0 - sig))
        dup = ga * silu
        n = gate.shape[1]
        part = pl.ds(at, n)
        d[0, :, part] = (silu * up).astype(BF)
        d[1, :, part] = dgate.astype(BF)
        d[2, :, part] = dup.astype(BF)
        turned[0, part, :] = dgate.T.astype(BF)
        turned[1, part, :] = dup.T.astype(BF)
        at += n
    rows, width = own.shape
    n = width // chunks

    @pl.loop(0, chunks)
    def _(c):
        cols = pl.ds(pl.multiple_of(c * n, n), n)
        s = jnp.dot(turned[0], wg[:, cols], preferred_element_type=F32)
        s += jnp.dot(turned[1], wu[:, cols], preferred_element_type=F32)
        own[:, cols] = s[:rows].astype(own.dtype)
        low = s[rows:]
        if joined:
            low += extra[:, cols].astype(F32) * keep[0].astype(F32)
        oth[:, cols] = low.astype(oth.dtype)


def act(arrays, pieces, wg, wu, rows, kinds, joined=()):
    hid, width = wg.shape
    return call(
        functools.partial(act_body, pieces, 5, len(joined)),
        (*joined, *arrays, wg, wu),
        [((3, hid, 2 * rows), BF)] + [((rows, width), t) for t in kinds],
        16 * rows * hid * width,
        scratch=[pltpu.VMEM((2, 2 * rows, hid), BF)],
        scalars=len(joined) // 2,
    )


def dw_body(chunks, odd, *refs):
    sources, (d1, d2, x0, g0, x1, g1, x2, g2, gg, gu, gd, buf, sems) = refs[:4], refs[4:]
    pick_copies(odd, sources, buf, sems)
    for i in range(2):
        pick_wait(sources, buf, sems, i)
    n = gg.shape[1] // chunks
    rows = x1.shape[0]
    top, low = pl.ds(0, rows), pl.ds(rows, rows)

    @pl.loop(0, chunks)
    def _(c):
        cols = pl.ds(pl.multiple_of(c * n, n), n)
        x = jnp.concatenate([x0[:, cols], x1[:, cols], x2[:, cols], buf[top, cols]], 0)
        g = jnp.concatenate([g0[:, cols], g1[:, cols], g2[:, cols], buf[low, cols]], 0)
        for i, out, t in ((1, gg, x), (2, gu, x), (0, gd, g)):
            d = jnp.concatenate([d1[i], d2[i]], 1)
            out[:, cols] = jnp.dot(d, t, preferred_element_type=F32).astype(BF)


def dw(odd, sources, d1, d2, tokens):
    hid = d1.shape[1]
    rows, width = sources[0].shape
    return call(
        functools.partial(dw_body, 5),
        (odd, *sources, d1, d2, *tokens),
        [((hid, width), BF)] * 3,
        24 * rows * hid * width,
        scratch=[pltpu.VMEM((2 * rows, width), BF), pltpu.SemaphoreType.DMA((2,))],
        scalars=1,
        raw=4,
    )


def last_body(where, own1, own2, left, flip, out):
    half = own1.shape[1]
    own = pl.ds(pl.multiple_of(where[1] * half, 128), half)
    oth = pl.ds(pl.multiple_of((1 - where[1]) * half, 128), half)
    out[:, own] = (own1[...] + own2[...].astype(F32)).astype(BF)

    @pl.when(where[0] == 1)
    def _():
        out[:, oth] = flip[...]

    @pl.when(where[0] == 0)
    def _():
        out[:, oth] = (left[...].astype(F32) + flip[...].astype(F32)).astype(BF)


def solution(mesh):
    route = routes(mesh.shape["blk"])

    def go(value, name):
        return lax.ppermute(value, AXES, route[name])

    def steps(inputs, upstream, w_gate_t, w_up_t, w_down):
        rows, width = inputs.shape
        half = width // 2
        weights = (w_gate_t, w_up_t, w_down)
        rep = lax.axis_index("rep").astype(jnp.int32)
        odd = (lax.axis_index("blk") % 2).astype(jnp.int32).reshape(1)
        cut = lambda a, at: lax.dynamic_slice(a, (0, at * half), (rows, half))
        x_snd, g_snd = cut(inputs, 1 - rep), cut(upstream, 1 - rep)
        x_own, g_own = (cut(a, rep) for a in lax.optimization_barrier((inputs, upstream)))
        x_oth, g_oth = go(x_snd, "swap"), go(g_snd, "swap")
        links = [go(x_snd, "back_flip"), go(g_snd, "back_flip")]
        p1_own, p1_own16 = pre([x_own, g_own], (0, 0, 1), weights)
        r1_oth = go(p1_own16, "swap")
        x2_own, g2_own = go(x_own, "back"), go(g_own, "back")
        p1_x, p1_x16 = pre([x_oth], (0, 0), weights[:2])
        p1_g, p1_g16 = pre([g_oth], (0,), weights[2:])
        r1_x, r1_g = go(p1_x16, "swap"), go(p1_g16, "swap")
        sources = (*links, go(x_oth, "same_chip"), go(g_oth, "same_chip"))
        three = lambda i: ((i, 0), (i, 1), (i, 2))
        split = lambda i: ((i, 0), (i, 1), (i + 1, 0))
        d1, own1, oth1 = act(
            (p1_own, r1_oth, p1_x, p1_g, r1_x, r1_g),
            ((three(0), split(4)), (split(2), three(1))),
            w_gate_t,
            w_up_t,
            rows,
            (F32, BF),
        )
        left = go(oth1, "swap_even")
        below = go(oth1, "same_chip")
        p2_oth, p2_oth16 = pre2oth(odd, sources, weights)
        r2_own = go(p2_oth16, "swap")
        p2_own, p2_own16 = pre([x2_own, g2_own], (0, 0, 1), weights)
        r2_oth = go(p2_own16, "swap")
        d2, own2, oth2 = act(
            (p2_own, p2_oth, r2_own, r2_oth),
            ((three(0), three(2)), (three(1), three(3))),
            w_gate_t,
            w_up_t,
            rows,
            (BF, BF),
            (1 - odd, below),
        )
        own2_home = go(own2, "fwd")
        flip = go(oth2, "fwd_flip")
        gg, gu, gd = dw(odd, sources, d1, d2, (x_own, g_own, x_oth, g_oth, x2_own, g2_own))
        (d_in,) = call(
            last_body,
            (jnp.stack([odd[0], rep]), own1, own2_home, left, flip),
            [((rows, width), BF)],
            2 * rows * width,
            scalars=1,
        )
        return d_in, gg, gu, gd

    tokens, weights = P(AXES, None), P("blk", "rep")
    return jax.shard_map(
        steps,
        mesh=mesh,
        in_specs=(tokens, tokens, weights, weights, weights),
        out_specs=(tokens, weights, weights, weights),
        check_vma=False,
    )
```

```python
import functools

import jax
import jax.numpy as jnp
from jax import lax
from jax.experimental import pallas as pl
from jax.experimental.pallas import tpu as pltpu
from jax.sharding import PartitionSpec as P

BF = jnp.bfloat16
F32 = jnp.float32
AXES = ("blk", "rep")
LAST = (((1,), (1,)), ((), ()))
IN_VMEM = pl.BlockSpec(memory_space=pltpu.VMEM)
IN_SMEM = pl.BlockSpec(memory_space=pltpu.SMEM)
IN_PLACE = pl.BlockSpec(memory_space=pltpu.HBM)


def routes(n_blk):
    def at(b, r):
        return (b % n_blk) * 2 + r

    every = [(b, r) for b in range(n_blk) for r in (0, 1)]
    return {
        "swap": [(at(b, r), at(b, 1 - r)) for b, r in every],
        "back": [(at(b, r), at(b - 1, r)) for b, r in every],
        "back_flip": [(at(b, r), at(b - 1, r if b % 2 else 1 - r)) for b, r in every],
        "same_chip": [(at(b, r), at(b ^ 1, r)) for b, r in every],
        "fwd": [(at(b, r), at(b + 1, r)) for b, r in every],
        "fwd_flip": [(at(b, r), at(b + 1, 1 - r)) for b, r in every],
        "swap_even": [(at(b, r), at(b, 1 - r)) for b, r in every if b % 2 == 0],
    }


def call(body, args, outs, flops, scratch=(), scalars=0, raw=0):
    shapes = [jax.ShapeDtypeStruct(s, k) for s, k in outs]
    nbytes = sum(a.size * a.dtype.itemsize for a in (*args, *shapes))
    specs = [IN_SMEM] * scalars + [IN_PLACE] * raw + [IN_VMEM] * (len(args) - scalars - raw)
    return pl.pallas_call(
        body,
        in_specs=specs,
        out_specs=[IN_VMEM] * len(shapes),
        out_shape=shapes,
        scratch_shapes=list(scratch),
        compiler_params=pltpu.CompilerParams(vmem_limit_bytes=nbytes + (4 << 20)),
        cost_estimate=pl.CostEstimate(flops=flops, bytes_accessed=nbytes, transcendentals=0),
    )(*args)


def pre_body(picks, *refs):
    n = max(picks) + 1
    tokens, ws, (out, out16) = refs[:n], refs[n:-2], refs[-2:]
    for i, (w, k) in enumerate(zip(ws, picks)):
        s = lax.dot_general(w[...], tokens[k][...], LAST, preferred_element_type=F32)
        out[i] = s
        out16[i] = s.astype(BF)


def pre(tokens, picks, weights):
    hid, width = weights[0].shape
    rows = tokens[0].shape[0]
    shape = (len(weights), hid, rows)
    return call(
        functools.partial(pre_body, picks),
        (*tokens, *weights),
        [(shape, F32), (shape, BF)],
        2 * len(weights) * rows * width * hid,
    )


def pick_copies(odd, sources, buf, sems):
    rows = sources[0].shape[0]
    for i in range(2):
        dst = buf.at[pl.ds(i * rows, rows)]

        @pl.when(odd[0] == 1)
        def _():
            pltpu.make_async_copy(sources[i], dst, sems.at[i]).start()

        @pl.when(odd[0] == 0)
        def _():
            pltpu.make_async_copy(sources[2 + i], dst, sems.at[i]).start()


def pick_wait(sources, buf, sems, i):
    rows = sources[0].shape[0]
    pltpu.make_async_copy(sources[i], buf.at[pl.ds(i * rows, rows)], sems.at[i]).wait()


def pre2oth_body(odd, *refs):
    sources, (wg, wu, wd, out, out16, buf, sems) = refs[:4], refs[4:]
    rows = sources[0].shape[0]
    pick_copies(odd, sources, buf, sems)
    for i, (w, p) in enumerate(((wg, 0), (wu, 0), (wd, 1))):
        if i != 1:
            pick_wait(sources, buf, sems, p)
        t = buf[p * rows : (p + 1) * rows]
        s = lax.dot_general(w[...], t, LAST, preferred_element_type=F32)
        out[i] = s
        out16[i] = s.astype(BF)


def pre2oth(odd, sources, weights):
    rows, width = sources[0].shape
    hid = weights[0].shape[0]
    shape = (3, hid, rows)
    return call(
        pre2oth_body,
        (odd, *sources, *weights),
        [(shape, F32), (shape, BF)],
        6 * rows * width * hid,
        scratch=[pltpu.VMEM((2 * rows, width), BF), pltpu.SemaphoreType.DMA((2,))],
        scalars=1,
        raw=4,
    )


def act_body(pieces, chunks, joined, *refs):
    if joined:
        keep, extra, *refs = refs
    wg, wu, d, own, oth, turned = refs[-6:]
    at = 0
    for ps, rs in pieces:
        gate, up, ga = (refs[i][j] + refs[k][m].astype(F32) for (i, j), (k, m) in zip(ps, rs))
        sig = 1.0 / (1.0 + jnp.exp(-gate))
        silu = gate * sig
        dgate = ga * up * sig * (1.0 + gate * (1.0 - sig))
        dup = ga * silu
        n = gate.shape[1]
        part = pl.ds(at, n)
        d[0, :, part] = (silu * up).astype(BF)
        d[1, :, part] = dgate.astype(BF)
        d[2, :, part] = dup.astype(BF)
        turned[0, part, :] = dgate.T.astype(BF)
        turned[1, part, :] = dup.T.astype(BF)
        at += n
    rows, width = own.shape
    n = width // chunks

    @pl.loop(0, chunks)
    def _(c):
        cols = pl.ds(pl.multiple_of(c * n, n), n)
        s = jnp.dot(turned[0], wg[:, cols], preferred_element_type=F32)
        s += jnp.dot(turned[1], wu[:, cols], preferred_element_type=F32)
        own[:, cols] = s[:rows].astype(own.dtype)
        low = s[rows:]
        if joined:
            low += extra[:, cols].astype(F32) * keep[0].astype(F32)
        oth[:, cols] = low.astype(oth.dtype)


def act(arrays, pieces, wg, wu, rows, kinds, joined=()):
    hid, width = wg.shape
    return call(
        functools.partial(act_body, pieces, 5, len(joined)),
        (*joined, *arrays, wg, wu),
        [((3, hid, 2 * rows), BF)] + [((rows, width), t) for t in kinds],
        16 * rows * hid * width,
        scratch=[pltpu.VMEM((2, 2 * rows, hid), BF)],
        scalars=len(joined) // 2,
    )


def dw_body(chunks, odd, *refs):
    sources, (d1, d2, x0, g0, x1, g1, x2, g2, gg, gu, gd, buf, sems) = refs[:4], refs[4:]
    pick_copies(odd, sources, buf, sems)
    for i in range(2):
        pick_wait(sources, buf, sems, i)
    n = gg.shape[1] // chunks
    rows = x1.shape[0]
    top, low = pl.ds(0, rows), pl.ds(rows, rows)

    @pl.loop(0, chunks)
    def _(c):
        cols = pl.ds(pl.multiple_of(c * n, n), n)
        x = jnp.concatenate([x0[:, cols], x1[:, cols], x2[:, cols], buf[top, cols]], 0)
        g = jnp.concatenate([g0[:, cols], g1[:, cols], g2[:, cols], buf[low, cols]], 0)
        for i, out, t in ((1, gg, x), (2, gu, x), (0, gd, g)):
            d = jnp.concatenate([d1[i], d2[i]], 1)
            out[:, cols] = jnp.dot(d, t, preferred_element_type=F32).astype(BF)


def dw(odd, sources, d1, d2, tokens):
    hid = d1.shape[1]
    rows, width = sources[0].shape
    return call(
        functools.partial(dw_body, 5),
        (odd, *sources, d1, d2, *tokens),
        [((hid, width), BF)] * 3,
        24 * rows * hid * width,
        scratch=[pltpu.VMEM((2 * rows, width), BF), pltpu.SemaphoreType.DMA((2,))],
        scalars=1,
        raw=4,
    )


def put(at, buf, out, sem):
    half = buf.shape[1]
    cols = pl.ds(pl.multiple_of(at * half, 128), half)
    copy = pltpu.make_async_copy(buf, out.at[:, cols], sem)
    copy.start()
    copy.wait()


def own_body(where, a, b, out, buf, sem):
    buf[...] = (a[...] + b[...].astype(F32)).astype(BF)
    put(where[1], buf, out, sem)


def oth_body(where, _, left, flip, out, buf, sem):
    @pl.when(where[0] == 1)
    def _():
        buf[...] = flip[...]

    @pl.when(where[0] == 0)
    def _():
        buf[...] = (left[...].astype(F32) + flip[...].astype(F32)).astype(BF)

    put(1 - where[1], buf, out, sem)


def half_out(body, where, args, shape, base=()):
    return pl.pallas_call(
        body,
        in_specs=[IN_SMEM] + [IN_PLACE] * len(base) + [IN_VMEM] * len(args),
        out_specs=IN_PLACE,
        out_shape=jax.ShapeDtypeStruct(shape, BF),
        scratch_shapes=[pltpu.VMEM(args[0].shape, BF), pltpu.SemaphoreType.DMA],
        input_output_aliases={1: 0} if base else {},
        compiler_params=pltpu.CompilerParams(vmem_limit_bytes=8 << 20),
    )(where, *base, *args)


def solution(mesh):
    route = routes(mesh.shape["blk"])

    def go(value, name):
        return lax.ppermute(value, AXES, route[name])

    def steps(inputs, upstream, w_gate_t, w_up_t, w_down):
        rows, width = inputs.shape
        half = width // 2
        weights = (w_gate_t, w_up_t, w_down)
        rep = lax.axis_index("rep").astype(jnp.int32)
        odd = (lax.axis_index("blk") % 2).astype(jnp.int32).reshape(1)
        cut = lambda a, at: lax.dynamic_slice(a, (0, at * half), (rows, half))
        x_snd, g_snd = cut(inputs, 1 - rep), cut(upstream, 1 - rep)
        x_own, g_own = (cut(a, rep) for a in lax.optimization_barrier((inputs, upstream)))
        x_oth, g_oth = go(x_snd, "swap"), go(g_snd, "swap")
        links = [go(x_snd, "back_flip"), go(g_snd, "back_flip")]
        p1_own, p1_own16 = pre([x_own, g_own], (0, 0, 1), weights)
        r1_oth = go(p1_own16, "swap")
        x2_own, g2_own = go(x_own, "back"), go(g_own, "back")
        p1_x, p1_x16 = pre([x_oth], (0, 0), weights[:2])
        p1_g, p1_g16 = pre([g_oth], (0,), weights[2:])
        r1_x, r1_g = go(p1_x16, "swap"), go(p1_g16, "swap")
        sources = (*links, go(x_oth, "same_chip"), go(g_oth, "same_chip"))
        three = lambda i: ((i, 0), (i, 1), (i, 2))
        split = lambda i: ((i, 0), (i, 1), (i + 1, 0))
        d1, own1, oth1 = act(
            (p1_own, r1_oth, p1_x, p1_g, r1_x, r1_g),
            ((three(0), split(4)), (split(2), three(1))),
            w_gate_t,
            w_up_t,
            rows,
            (F32, BF),
        )
        left = go(oth1, "swap_even")
        below = go(oth1, "same_chip")
        p2_oth, p2_oth16 = pre2oth(odd, sources, weights)
        r2_own = go(p2_oth16, "swap")
        p2_own, p2_own16 = pre([x2_own, g2_own], (0, 0, 1), weights)
        r2_oth = go(p2_own16, "swap")
        d2, own2, oth2 = act(
            (p2_own, p2_oth, r2_own, r2_oth),
            ((three(0), three(2)), (three(1), three(3))),
            w_gate_t,
            w_up_t,
            rows,
            (BF, BF),
            (1 - odd, below),
        )
        own2_home = go(own2, "fwd")
        flip = go(oth2, "fwd_flip")
        gg, gu, gd = dw(odd, sources, d1, d2, (x_own, g_own, x_oth, g_oth, x2_own, g2_own))
        where = jnp.stack([odd[0], rep])
        d_in = half_out(own_body, where, (own1, own2_home), (rows, width))
        d_in = half_out(oth_body, where, (left, flip), (rows, width), (d_in,))
        return d_in, gg, gu, gd

    tokens, weights = P(AXES, None), P("blk", "rep")
    return jax.shard_map(
        steps,
        mesh=mesh,
        in_specs=(tokens, tokens, weights, weights, weights),
        out_specs=(tokens, weights, weights, weights),
        check_vma=False,
    )
```
